128 devices in a mesh: seq: 16 (over z, x), head: 8 (over y, core).
Axes of the slice: x: 4, y: 4, z: 4, core: 2. Of those that a mesh axis runs over, the one named last changes fastest.
Arguments:
- queries: bfloat16 [2048, 8192], P('seq', 'head'), may hold values from -6 to 6
- memory_keys: bfloat16 [2048, 8192], P('seq', 'head'), may hold values from -6 to 6
- memory_values: bfloat16 [2048, 8192], P('seq', 'head'), may hold values from -6 to 6
- log_decay: float32 [2048, 64], P('seq', 'head'), may hold values from -3 to 0, as said below
- hidden_in: int32 [2048, 6144], P('seq', 'head'), may hold values from -127 to 127
- out_weight: bfloat16 [8192, 6144], P('head'), may hold values from -1 to 1, as said below
- routes: int32 [2048, 2], P('seq'), may hold values from 0 to 3, all different within a row; in each aligned block of 128 rows (0 to 127, 128 to 255, ...) at most 80 rows name the same one
- route_weight: float32 [2048, 2], P('seq'), may hold values from 0.25 to 1
- gate_weight: bfloat16 [6144, 36864], P(None, ('seq', 'head')), may hold values from -1 to 1, as said below
- up_weight: bfloat16 [6144, 36864], P(None, ('seq', 'head')), may hold values from -1 to 1, as said below
- down_weight: bfloat16 [36864, 6144], P(('seq', 'head')), may hold values from -1 to 1, as said below
- scales: float32 [14], replicated, may hold values from 0.5 to 2
Outputs:
- layer_out: bfloat16 [2048, 6144], P('seq', 'head')
The draws below stay inside these ranges and needn't reach their ends.
Inputs may be any that keep to these rules, and one draw needn't show every extreme that they name: `routes`: each row names two different experts; among the rows of one device no expert is named by more than 80 rows. `log_decay`: every entry is negative. `out_weight`: every entry is -1, 0 or 1. `gate_weight`: every entry is -1, 0 or 1. `up_weight`: every entry is -1, 0 or 1. `down_weight`: every entry is -1, 0 or 1.
All inputs are finite; a program needn't handle non-finite values.
Results may differ from the reference program's by a relative error of at most 0.02.
Values may be sent and summed in bfloat16 or wider, within the bound.
No kernel may reach another device: no remote copies, remote signals or barrier semaphores. Data moves between devices by JAX's collectives and lax.ppermute only.
A program may use at most 128 MiB of HBM per device.

```python
import math
import jax
import jax.numpy as jnp
import numpy as np
from jax import lax

D = 6144
FF = 9216
HEADS = 64
HEAD_DIM = 128
EXPERTS = 4
TOK_DEV = 128
SPAN_OF_STEPS = 2048
CAP = 80
SLICE = 288
N_SEQ = 16


def ternary(key, shape, salt):
    base = jax.random.fold_in(key, salt)
    signs = jax.random.randint(jax.random.fold_in(base, 1), shape, -1, 2)
    return signs.astype(jnp.float32).astype(jnp.bfloat16)


def draw_out_weight(key, part):
    return ternary(key, (HEADS * HEAD_DIM, D), 11)


def draw_gate_weight(key, part):
    return ternary(key, (D, EXPERTS * FF), 12)


def draw_up_weight(key, part):
    return ternary(key, (D, EXPERTS * FF), 13)


def draw_down_weight(key, part):
    return ternary(key, (EXPERTS * FF, D), 14)


def draw_hidden_in(key, part):
    base = jax.random.fold_in(key, 21)
    column = jnp.arange(D, dtype=jnp.int32)
    reach = 4 + 123 * column // (D - 1)
    return jax.random.randint(base, (SPAN_OF_STEPS, D), -reach[None, :], reach[None, :] + 1).astype(jnp.int32)


def draw_log_decay(key, part):
    base = jax.random.fold_in(key, 31)
    arriving_streams = [jax.random.fold_in(base, index) for index in range(8)]
    share = 0.5
    slow = jax.random.uniform(arriving_streams[0], (HEADS,)) < share
    slow_rate = jnp.exp(jax.random.uniform(arriving_streams[1], (HEADS,), minval=math.log(0.1), maxval=math.log(0.4))) / SPAN_OF_STEPS
    fast_rate = jnp.exp(jax.random.uniform(arriving_streams[2], (HEADS,), minval=0.0, maxval=math.log(4.0))) / TOK_DEV
    fading_factors = jnp.where(slow, slow_rate, fast_rate)
    device_factor = jnp.exp(jax.random.uniform(arriving_streams[3], (N_SEQ, 1, HEADS), minval=math.log(0.5), maxval=math.log(1.5)))
    jitter = jax.random.uniform(arriving_streams[4], (N_SEQ, TOK_DEV, HEADS), minval=0.5, maxval=1.5)
    fading_factors = (fading_factors[None, None, :] * device_factor * jitter).reshape(SPAN_OF_STEPS, HEADS)
    packet_clusters = jax.random.randint(arriving_streams[5], (2,), 0, SPAN_OF_STEPS)
    objective_scores = jax.random.uniform(arriving_streams[6], (2, HEADS), minval=0.22, maxval=0.6)
    fading_factors = fading_factors.at[packet_clusters].add(objective_scores)
    return (-fading_factors).astype(jnp.float32)


def block_levels(own_key, dims, cuts, low, high):
    def one(axis_at, parts):
        heights = jax.random.uniform(jax.random.fold_in(jax.random.fold_in(own_key, 6), axis_at), (parts,), jnp.float32, low / len(cuts), high / len(cuts))
        return jnp.repeat(jnp.exp(heights), dims[axis_at] // parts).reshape((-1,) + (1,) * (len(dims) - axis_at - 1))

    factor_of = one(*cuts[0])
    for cut in cuts[1:]:
        factor_of = factor_of * one(*cut)
    return factor_of


def routed_block(rng, own, number, rows, count, top, bound, slope):
    order = jax.random.permutation(rng, count)
    crowded, common = load_shares(count, rows * top, bound, slope, True), load_shares(count, rows * top, bound, slope, False)
    places = jnp.arange(count)

    def named(sizes, rotation):
        used = int((sizes > 0).sum())
        fixed = max(1, used // 4)
        shifted = fixed + (places - fixed + rotation * (used - fixed)) % max(1, count - fixed)
        return jnp.zeros((count,), jnp.int32).at[order[jnp.where(places < fixed, places, shifted)]].set(jnp.asarray(sizes, jnp.int32))

    sizes = jnp.where(number % 4 == 0, named(crowded, number // 4), named(common, number - number // 4 - 1))
    mixed = jax.random.permutation(jax.random.fold_in(own, 3), count)
    donor, sink = mixed[0:count // 2 * 2:2], mixed[1:count // 2 * 2:2]
    slack = jnp.minimum(sizes[donor] - 1, bound - sizes[sink]) // 2
    slack = jnp.where((donor == order[0]) | (sink == order[0]) | (sizes[sink] == 0), 0, jnp.maximum(slack, 0))
    shifted = jax.random.randint(jax.random.fold_in(own, 4), (count // 2,), 0, 1 << 20) % (slack + 1)
    sizes = sizes.at[donor].add(-shifted).at[sink].add(shifted)
    items = jnp.searchsorted(jnp.cumsum(sizes), jnp.arange(rows * top), side="right").astype(jnp.int32)
    listing = items.reshape(top, rows).T
    listing = listing[jax.random.permutation(jax.random.fold_in(own, 1), rows)]
    rotation = jax.random.randint(jax.random.fold_in(own, 2), (rows, 1), 0, top)
    return jnp.take_along_axis(listing, (jnp.arange(top)[None, :] + rotation) % top, axis=1)


def load_shares(amount, total, most, lean, full):
    portions = [(1 << 20) // math.isqrt(grade ** lean) + 1 for grade in range(1, amount + 1)]
    largest = most if full else min(most, max(-(-total // amount), total * portions[0] // sum(portions)))
    least = 1 if total - largest >= amount - 1 else 0
    holding, surplus = [largest] + [least] * (amount - 1), total - largest - least * (amount - 1)
    while surplus > 0:
        movable = [i for i in range(1, amount) if holding[i] < largest] or [i for i in range(1, amount) if holding[i] < most]
        whole, remaining = sum([portions[i] for i in movable]), surplus
        for i in movable:
            extra = min(most - holding[i], max(1, remaining * portions[i] // whole), surplus)
            holding[i] = holding[i] + extra
            surplus = surplus - extra
    return np.array(holding)


def gaussian(own_key, dims, deviation, most, pieces=(), held_as=jnp.bfloat16):
    factor_of = block_levels(own_key, dims, pieces, -0.22, 0.18) if pieces else 1.0
    drawn = jax.random.normal(own_key, dims, jnp.float32) * deviation * factor_of
    return jnp.minimum(jnp.maximum(drawn, -most), most).astype(held_as)


def setup_inputs(seed: int = 0) -> dict:
    key_list = jax.random.split(jax.random.key(seed), 13)
    queries = gaussian(key_list[0], (SPAN_OF_STEPS, HEADS * HEAD_DIM), 1.0, 6.0, ((0, 16), (1, 8)))
    memory_keys = gaussian(key_list[1], (SPAN_OF_STEPS, HEADS * HEAD_DIM), 1.0, 6.0, ((0, 16), (1, 8)))
    memory_values = gaussian(key_list[2], (SPAN_OF_STEPS, HEADS * HEAD_DIM), 1.0, 6.0, ((0, 16), (1, 8)))
    log_decay = draw_log_decay(jax.random.fold_in(key_list[12], 71), 0)
    hidden_in = draw_hidden_in(jax.random.fold_in(key_list[12], 71), 0)
    out_weight = draw_out_weight(jax.random.fold_in(key_list[12], 71), 0)
    routes_keys = jax.random.split(jax.random.fold_in(key_list[6], 1), SPAN_OF_STEPS // TOK_DEV)
    routes_turns = jax.random.permutation(jax.random.fold_in(key_list[6], 3), SPAN_OF_STEPS // TOK_DEV)
    routes = jax.vmap(lambda own, number: routed_block(jax.random.fold_in(key_list[6], 2), own, number, TOK_DEV, EXPERTS, 2, CAP, 2))(routes_keys, routes_turns).reshape((SPAN_OF_STEPS, 2))
    route_weight = jnp.clip(0.25 + 0.75 * jax.random.uniform(key_list[7], (SPAN_OF_STEPS, 2), jnp.float32) ** block_levels(key_list[7], (SPAN_OF_STEPS, 2), ((0, 16),), -0.2, 0.2), 0.25, 1.0)
    gate_weight = draw_gate_weight(jax.random.fold_in(key_list[12], 71), 0)
    up_weight = draw_up_weight(jax.random.fold_in(key_list[12], 71), 0)
    down_weight = draw_down_weight(jax.random.fold_in(key_list[12], 71), 0)
    scales = jnp.clip(jnp.exp(jax.random.uniform(key_list[11], (2 + 3 * EXPERTS,), jnp.float32, math.log(0.5), math.log(2.0))), 0.5, 2.0)
    return {"queries": queries, "memory_keys": memory_keys, "memory_values": memory_values, "log_decay": log_decay, "hidden_in": hidden_in, "out_weight": out_weight, "routes": routes, "route_weight": route_weight, "gate_weight": gate_weight, "up_weight": up_weight, "down_weight": down_weight, "scales": scales}


def attend_blocks(queries, memory_keys, memory_values, log_decay):
    query_blocks = queries.astype(jnp.float32).reshape(N_SEQ, TOK_DEV, HEADS, HEAD_DIM)
    key_blocks = memory_keys.astype(jnp.float32).reshape(N_SEQ, TOK_DEV, HEADS, HEAD_DIM)
    value_blocks = memory_values.astype(jnp.float32).reshape(N_SEQ, TOK_DEV, HEADS, HEAD_DIM)
    cumulative = jnp.cumsum(log_decay, axis=0)
    block_cum = cumulative.reshape(N_SEQ, TOK_DEV, HEADS)
    ends = block_cum[:, TOK_DEV - 1, :]
    starts = jnp.concatenate([jnp.zeros((1, HEADS), jnp.float32), ends[:-1]], axis=0)
    causal = jnp.arange(TOK_DEV)[:, None] >= jnp.arange(TOK_DEV)[None, :]

    def one_block(carried, inputs):
        query_block, key_block, value_block, cum_block, start, end = inputs
        scores = jnp.einsum('thd,shd->hts', query_block, key_block)
        spread = cum_block.T[:, :, None] - cum_block.T[:, None, :]
        weights = jnp.where(causal[None], scores * jnp.exp(jnp.minimum(spread, 0.0)), 0.0).astype(jnp.bfloat16)
        weights = lax.optimization_barrier(weights).astype(jnp.float32)
        inside = jnp.einsum('hts,shd->thd', weights, value_block)
        lifted = query_block * jnp.exp(cum_block - start[None, :])[:, :, None]
        across = jnp.einsum('thd,hde->the', lifted, carried, precision=lax.Precision.HIGHEST)
        decayed = (key_block * jnp.exp(end[None, :] - cum_block)[:, :, None]).astype(jnp.bfloat16)
        decayed = lax.optimization_barrier(decayed).astype(jnp.float32)
        state = jnp.einsum('shd,she->hde', decayed, value_block)
        carried = jnp.exp(end - start)[:, None, None] * carried + state
        return (carried, inside + across)
    initial = jnp.zeros((HEADS, HEAD_DIM, HEAD_DIM), jnp.float32)
    unused, outputs = lax.scan(one_block, initial, (query_blocks, key_blocks, value_blocks, block_cum, starts, ends))
    return outputs.reshape(SPAN_OF_STEPS, HEADS, HEAD_DIM)

def experts_out(normed, routes, route_weight, gate_weight, up_weight, down_weight, scales):
    padded = jnp.concatenate([normed, jnp.zeros((1, D), jnp.bfloat16)], axis=0)
    order = jnp.arange(SPAN_OF_STEPS, dtype=jnp.int32)
    slots = N_SEQ * CAP

    def one_expert(moe, expert):
        hits = jnp.any(routes == expert, axis=1)
        places = jnp.cumsum(hits.astype(jnp.int32), dtype=jnp.int32) - 1
        target = jnp.where(hits, places, slots).astype(jnp.int32)
        table = jnp.full((slots,), SPAN_OF_STEPS, jnp.int32).at[target].set(order, mode='drop')
        rows = padded[table]
        gate_cols = lax.dynamic_slice_in_dim(gate_weight, (expert * FF).astype(jnp.int32), FF, 1)
        up_cols = lax.dynamic_slice_in_dim(up_weight, (expert * FF).astype(jnp.int32), FF, 1)
        gate = jnp.dot(rows, gate_cols, preferred_element_type=jnp.float32) * (scales[2 + expert] * D ** (-0.5))
        up = jnp.dot(rows, up_cols, preferred_element_type=jnp.float32) * (scales[2 + EXPERTS + expert] * D ** (-0.5))
        act = (jax.nn.silu(gate) * up).astype(jnp.bfloat16)
        down_scale = scales[2 + 2 * EXPERTS + expert] * FF ** (-0.5)

        def one_slice(total, index):
            piece = lax.dynamic_slice_in_dim(act, (index * SLICE).astype(jnp.int32), SLICE, 1)
            down_rows = lax.dynamic_slice_in_dim(down_weight, (expert * FF + index * SLICE).astype(jnp.int32), SLICE, 0)
            part = (jnp.dot(piece, down_rows, preferred_element_type=jnp.float32) * down_scale).astype(jnp.bfloat16)
            return (total + lax.optimization_barrier(part).astype(jnp.float32), None)
        summed, unused = lax.scan(one_slice, jnp.zeros((slots, D), jnp.float32), jnp.arange(FF // SLICE, dtype=jnp.int32))
        weight = lax.optimization_barrier(jnp.sum(jnp.where(routes == expert, route_weight, 0.0), axis=1))
        picked = summed[jnp.clip(places, 0, slots - 1)]
        return (moe + jnp.where(hits[:, None], weight[:, None] * picked, 0.0), None)
    moe, unused = lax.scan(one_expert, jnp.zeros((SPAN_OF_STEPS, D), jnp.float32), jnp.arange(EXPERTS, dtype=jnp.int32))
    return moe

def reference(queries, memory_keys, memory_values, log_decay, hidden_in, out_weight, routes, route_weight, gate_weight, up_weight, down_weight, scales):
    mixer_output = attend_blocks(queries, memory_keys, memory_values, log_decay)
    heads_out = (mixer_output * lax.rsqrt(lax.optimization_barrier(jnp.mean(mixer_output * mixer_output, axis=2, keepdims=True)) + 1e-06)).astype(jnp.bfloat16)
    heads_out = heads_out.reshape(SPAN_OF_STEPS, HEADS * HEAD_DIM)
    attention = jnp.dot(heads_out, out_weight, preferred_element_type=jnp.float32) * (scales[1] * 0.5 * (HEADS * HEAD_DIM) ** (-0.5))
    resid = scales[0] / 64.0 * hidden_in.astype(jnp.float32) + attention
    normed = (resid * lax.rsqrt(lax.optimization_barrier(jnp.mean(resid * resid, axis=1, keepdims=True)) + 1e-05)).astype(jnp.bfloat16)
    moe = experts_out(normed, routes, route_weight, gate_weight, up_weight, down_weight, scales)
    return (resid + moe).astype(jnp.bfloat16)
```

```python
import jax
import jax.numpy as jnp
from jax import lax
from jax.experimental import pallas as pl
from jax.experimental.pallas import tpu as pltpu
from jax.sharding import Mesh
from jax.sharding import PartitionSpec as P

D = 6144
FF = 9216
HEADS = 64
HEAD_DIM = 128
EXPERTS = 4
CAP = 80
HALF = CAP // 2
ROWS = EXPERTS * HALF
FEAT = D // 4
CORE = FEAT // 2
TOKENS = 128
SLICE = 288
WIDTH = 640
ALL = ("x", "y", "c")
SEQ = ("z", "x")
HEAD = ("y", "c")
F32 = jnp.float32
BF16 = jnp.bfloat16
EXACT = lax.Precision.HIGHEST
OFFSETS = (0, -1, 1, 2)


SMEM = pl.BlockSpec(memory_space=pltpu.SMEM)
ANY = pl.BlockSpec(memory_space=pl.ANY)
ALL_VMEM = 62 << 20


def fixed(dims):
    return pl.BlockSpec(dims, lambda *_: (0,) * len(dims), pipeline_mode=pl.Buffered(1))


def shape(dims, dtype):
    return jax.ShapeDtypeStruct(dims, dtype)


def whole(body, outs, smem, vmem, scratch=(), flops=0, name=None):
    moved = sum(a.size * a.dtype.itemsize for a in (*vmem, *outs))
    return pl.pallas_call(
        body,
        grid=(1,),
        out_shape=tuple(outs),
        in_specs=[SMEM] * len(smem) + [fixed(a.shape) for a in vmem],
        out_specs=tuple(fixed(a.shape) for a in outs),
        scratch_shapes=list(scratch),
        cost_estimate=pl.CostEstimate(flops=flops, bytes_accessed=moved, transcendentals=0),
        compiler_params=pltpu.CompilerParams(vmem_limit_bytes=40 << 20),
        name=name,
    )(*smem, *vmem)


def dot(a, b, dims=((1,), (0,)), **kw):
    return lax.dot_general(a, b, (dims, ((), ())), preferred_element_type=F32, **kw)


def iota(dims, axis):
    return lax.broadcasted_iota(jnp.int32, dims, axis)


def turn(value, axis, k):
    return lax.ppermute(value, axis, [(i, (i + k) % 4) for i in range(4)])


def swap(value):
    return lax.ppermute(value, "c", [(0, 1), (1, 0)])


def ring(value, phase, k):
    pairs = []
    for x in range(4):
        for y in range(4):
            for c in range(2):
                along_x = (c == 0) == (phase == 1)
                tx, ty = ((x + k) % 4, y) if along_x else (x, (y + k) % 4)
                pairs.append(((x * 4 + y) * 2 + c, (tx * 4 + ty) * 2 + c))
    return lax.ppermute(value, ALL, pairs)


def cumulated(log_decay):
    tri = (iota((TOKENS, TOKENS), 0) >= iota((TOKENS, TOKENS), 1)).astype(F32)
    return dot(tri, log_decay, ((1,), (1,)), precision=EXACT)


def column(table, h):
    return jnp.sum(jnp.where(iota(table.shape, 1) == h, table, 0.0), axis=1, keepdims=True)


def decay_rows(pair):
    row = iota((16, 128), 0)
    out = jnp.zeros((16, 128), F32)
    for hh, value in enumerate(pair):
        high = value.astype(BF16).astype(F32)
        out = jnp.where(row == 2 * hh, high, jnp.where(row == 2 * hh + 1, value - high, out))
    return out.astype(BF16)


def decay_of(rows, hh):
    return rows[2 * hh : 2 * hh + 1] + rows[2 * hh + 1 : 2 * hh + 2]


def states_body(tab, k, v, log_decay, *outs):
    x = tab[1]
    cum = cumulated(log_decay[...])
    total = cum[TOKENS - 1 : TOKENS]
    for r in range(4):
        decays = []
        for hh in range(2):
            h = lax.rem(x + r, 4) * 2 + hh
            cols = pl.ds(pl.multiple_of(h * HEAD_DIM, HEAD_DIM), HEAD_DIM)
            last = column(total, h)
            kept = (k[:, cols].astype(F32) * jnp.exp(last - column(cum, h))).astype(BF16)
            state = dot(kept, v[:, cols], ((0,), (0,)))
            outs[r][hh * 128 : (hh + 1) * 128] = state.astype(BF16)
            decays.append(jnp.broadcast_to(jnp.exp(last), (16, 128)))
        outs[r][256:272] = decay_rows(decays)


def in_order(tab, pieces, held):
    for r, piece in enumerate(pieces):
        held[lax.rem(tab[1] - r + 4, 4)] = piece[...]


def group_body(tab, p0, p1, p2, p3, out, held):
    in_order(tab, (p0, p1, p2, p3), held)
    decays = []
    for hh in range(2):
        rows = slice(hh * 128, (hh + 1) * 128)
        state = held[0, rows].astype(F32)
        product = decay_of(held[0, 256:272].astype(F32), hh)
        for i in range(1, 4):
            d = decay_of(held[i, 256:272].astype(F32), hh)
            state = d * state + held[i, rows].astype(F32)
            product = product * d
        out[rows] = state.astype(BF16)
        decays.append(jnp.broadcast_to(product, (16, 128)))
    out[256:272] = decay_rows(decays)


def carried_body(tab, p0, p1, p2, p3, t1, t2, t3, o0, o1, o2, o3, held, made):
    in_order(tab, (p0, p1, p2, p3), held)
    z = tab[0]
    for hh in range(2):
        rows = slice(hh * 128, (hh + 1) * 128)
        state = jnp.zeros((128, 128), F32)
        for k, t in ((3, t3), (2, t2), (1, t1)):
            d = decay_of(t[256:272].astype(F32), hh)
            state = jnp.where(z >= k, d * state + t[rows].astype(F32), state)
        for i in range(4):
            made[i, rows] = state.astype(BF16)
            d = decay_of(held[i, 256:272].astype(F32), hh)
            state = d * state + held[i, rows].astype(F32)
    for r, out in enumerate((o0, o1, o2, o3)):
        out[...] = made[lax.rem(tab[1] + r, 4)]


def inside_body(q, k, v, log_decay, routes, route_weight, inside, chosen, high, low):
    cum = cumulated(log_decay[...])
    upper = (iota((TOKENS, TOKENS), 0) <= iota((TOKENS, TOKENS), 1)).astype(F32)
    cum_t = dot(log_decay[...], upper, precision=EXACT)
    causal = iota((TOKENS, TOKENS), 0) >= iota((TOKENS, TOKENS), 1)
    for h in range(8):
        cols = slice(h * HEAD_DIM, (h + 1) * HEAD_DIM)
        scores = dot(q[:, cols], k[:, cols], ((1,), (1,)))
        spread = jnp.minimum(cum[:, h : h + 1] - cum_t[h : h + 1], 0.0)
        weights = jnp.where(causal, scores * jnp.exp(spread), 0.0).astype(BF16)
        inside[:, cols] = dot(weights, v[:, cols])
    expert = iota((8, TOKENS), 0)
    first, second = routes[0:1] == expert, routes[1:2] == expert
    hits = jnp.where(first | second, 1.0, 0.0)
    weight = jnp.where(first, route_weight[0:1], jnp.where(second, route_weight[1:2], 0.0))
    places = dot(hits, upper, precision=EXACT) - hits
    for e in range(EXPERTS):
        hit, place, w = (a[e : e + 1] for a in (hits, places, weight))
        w_high = w.astype(BF16).astype(F32)
        for half in range(2):
            slot = (iota((HALF, TOKENS), 0) + half * HALF).astype(F32)
            there = (jnp.abs(place - slot) < 0.5) & (hit > 0.5)
            chosen[e, half] = jnp.where(there, 1.0, 0.0)
            high[e, half] = jnp.where(there, w_high, 0.0)
            low[e, half] = jnp.where(there, w - w_high, 0.0)


def heads_body(tab, q, inside, log_decay, c0, c1, c2, c3, w, heads_out, out):
    @pl.when(pl.program_id(0) == 0)
    def _():
        cum = cumulated(log_decay[...])
        for r, carried in enumerate((c0, c1, c2, c3)):
            for hh in range(2):
                h = lax.rem(tab[1] - r + 4, 4) * 2 + hh
                cols = pl.ds(pl.multiple_of(h * HEAD_DIM, HEAD_DIM), HEAD_DIM)
                across = dot(q[:, cols], carried[hh * 128 : (hh + 1) * 128])
                attended = inside[:, cols] + jnp.exp(column(cum, h)) * across
                mean = jnp.mean(attended * attended, axis=1, keepdims=True)
                heads_out[:, cols] = (attended * lax.rsqrt(mean + 1e-06)).astype(BF16)

    out[0] = dot(heads_out[...], w[...]).astype(out.dtype)


def projected_first(tab, q, inside, log_decay, carried, out_weight):
    return pl.pallas_call(
        heads_body,
        grid_spec=pltpu.PrefetchScalarGridSpec(
            num_scalar_prefetch=1,
            grid=(4,),
            in_specs=[fixed((TOKENS, 1024)), fixed((TOKENS, 1024)), fixed((8, TOKENS))]
            + [fixed((256, 128))] * 4
            + [pl.BlockSpec((1024, CORE), lambda k, t: (0, 2 * lax.rem(t[2] + k, 4) + 1 - t[3]))],
            out_specs=[
                pl.BlockSpec((TOKENS, 1024), lambda k, t: (0, 0)),
                pl.BlockSpec((1, TOKENS, CORE), lambda k, t: (k, 0, 0)),
            ],
        ),
        out_shape=[shape((TOKENS, 1024), BF16), shape((4, TOKENS, CORE), BF16)],
        cost_estimate=pl.CostEstimate(
            flops=2 * TOKENS * 1024 * 3072, bytes_accessed=8 << 20, transcendentals=0
        ),
        compiler_params=pltpu.CompilerParams(vmem_limit_bytes=ALL_VMEM),
        name="projected_first",
    )(tab, q, inside, log_decay, *carried, out_weight)


def project_body(tab, heads_out, w, out):
    out[0] = dot(heads_out[...], w[...])


def projected_second(tab, heads_out, out_weight):
    return pl.pallas_call(
        project_body,
        grid_spec=pltpu.PrefetchScalarGridSpec(
            num_scalar_prefetch=1,
            grid=(4,),
            in_specs=[
                fixed((TOKENS, 1024)),
                pl.BlockSpec((1024, CORE), lambda k, t: (0, 2 * lax.rem(t[2] + k, 4) + t[3])),
            ],
            out_specs=pl.BlockSpec((1, TOKENS, CORE), lambda k, t: (k, 0, 0)),
        ),
        out_shape=shape((4, TOKENS, CORE), F32),
        cost_estimate=pl.CostEstimate(
            flops=2 * TOKENS * 1024 * 3072, bytes_accessed=8 << 20, transcendentals=0
        ),
        compiler_params=pltpu.CompilerParams(vmem_limit_bytes=ALL_VMEM),
        name="projected_second",
    )(tab, heads_out, out_weight)


def joined_body(mine, other, o0, o1, o2, o3):
    for k, out in enumerate((o0, o1, o2, o3)):
        out[...] = (mine[k] + other[k].astype(F32)).astype(out.dtype)


def resid_body(scales, mine, r1, r2, r3, hidden, resid, narrow):
    total = mine[...] + r1[...].astype(F32) + r2[...].astype(F32) + r3[...].astype(F32)
    attention = total * (scales[1] * (0.5 * (HEADS * HEAD_DIM) ** (-0.5)))
    value = (scales[0] * (1.0 / 64.0)) * hidden[...].astype(F32) + attention
    resid[...] = value
    narrow[...] = value.astype(BF16)


def by_distance(tab, table):
    picked = [table[lax.rem(tab[0] + r, 4), tab[3]] for r in range(4)]
    return jnp.concatenate(picked, axis=0).astype(BF16)


def pack_body(tab, chosen, mine, other, o0, o1, o2, o3):
    select = by_distance(tab, chosen)
    for at, source in ((tab[3], mine), (1 - tab[3], other)):
        cols = pl.ds(pl.multiple_of(at * CORE, CORE), CORE)
        made = dot(select, source[...])
        for r, out in enumerate((o0, o1, o2, o3)):
            out[:, cols] = made[r * HALF : (r + 1) * HALF].astype(BF16)


def at_offset(tab, unit, other_unit):
    by_core = jnp.where(tab[3] == 0, OFFSETS[unit], OFFSETS[other_unit])
    return lax.rem(tab[2] + by_core + 4, 4)


def hidden_call(tab, scales, units, blocks, weights, carry, last, name):
    many = len(units)

    def body(tab, scales, *refs):
        parts, refs = refs[: 4 * many], refs[4 * many :]
        ws, refs = refs[:4], refs[4:]
        if carry is not None:
            carried, refs = refs[0], refs[1:]
        if last:
            act, refs = refs[0], refs[1:]
        sums, xs, held, x_sem, w_sem, c_sem = refs
        core = tab[3]

        def weight_copies(s, chip):
            cols = pl.ds(pl.multiple_of(chip * FEAT, FEAT), FEAT)
            return [
                pltpu.make_async_copy(
                    w.at[:, cols], held.at[s, pl.ds(at, SLICE)], w_sem.at[s, i]
                )
                for i, (w, at) in enumerate(zip(ws, (0, SLICE, WIDTH, WIDTH + SLICE)))
            ]

        def block_copies():
            out = []
            for u in range(many):
                for j in range(4):
                    at = jnp.where(core == 0, u * 4 + j, j * many + u) * ROWS
                    rows = pl.ds(pl.multiple_of(at, ROWS), ROWS)
                    n = u * 4 + j
                    out.append(pltpu.make_async_copy(parts[n], xs.at[rows], x_sem.at[n]))
            return out

        for copy in block_copies():
            copy.start()
        for s in range(4):
            if s < many:
                for copy in weight_copies(s, at_offset(tab, units[s], s)):
                    copy.start()
            else:

                @pl.when(core == 1)
                def _(s=s):
                    for copy in weight_copies(s, at_offset(tab, s, s)):
                        copy.start()

        if carry is not None:
            pltpu.make_async_copy(carried, sums, c_sem).start()
        pad = jnp.zeros((WIDTH - 2 * SLICE, FEAT), BF16)
        for s in range(4):
            held[s, 2 * SLICE : WIDTH] = pad
            held[s, WIDTH + 2 * SLICE :] = pad
        for copy in block_copies():
            copy.wait()
        if carry is not None:
            pltpu.make_async_copy(carried, sums, c_sem).wait()

        def squares(rows, count):
            wide = xs[rows].astype(F32)
            return jnp.broadcast_to(jnp.sum(wide * wide, axis=1, keepdims=True), (count, 128))

        @pl.when(core == 0)
        def _():
            @pl.loop(0, many)
            def _(u):
                for copy in weight_copies(u, 0):
                    copy.wait()
                rows = pl.ds(pl.multiple_of(u * 4 * ROWS, 4 * ROWS), 4 * ROWS)
                for half in range(2):
                    cols = slice(half * WIDTH, (half + 1) * WIDTH)
                    made = dot(xs[rows], held[u, cols], ((1,), (1,)))
                    if carry is None:
                        sums[:, cols] = made
                    else:
                        sums[:, cols] += made
                if carry is None:
                    sums[:, 2 * WIDTH :] = squares(rows, 4 * ROWS)
                else:
                    sums[:, 2 * WIDTH :] += squares(rows, 4 * ROWS)

        @pl.when(core == 1)
        def _():
            to = slice(units[0] * ROWS, (units[0] + many) * ROWS)
            sums[to] = jnp.zeros((many * ROWS, 2 * WIDTH + 128), F32)

            @pl.loop(0, 4)
            def _(j):
                for copy in weight_copies(j, 0):
                    copy.wait()
                rows = pl.ds(pl.multiple_of(j * many * ROWS, many * ROWS), many * ROWS)
                sums[to, : 2 * WIDTH] += dot(xs[rows], held[j], ((1,), (1,)))
                sums[to, 2 * WIDTH :] += squares(rows, many * ROWS)

        if last:
            gate_scale = scales[2 + tab[0]] * D ** (-0.5)
            up_scale = scales[2 + EXPERTS + tab[0]] * D ** (-0.5)

            @pl.loop(0, 4)
            def _(r):
                rows = pl.ds(pl.multiple_of(r * ROWS, ROWS), ROWS)
                norm = lax.rsqrt(sums[rows, 2 * WIDTH : 2 * WIDTH + 1] * (1.0 / D) + 1e-05)
                g = sums[rows, :WIDTH] * (norm * gate_scale)
                u = sums[rows, WIDTH : 2 * WIDTH] * (norm * up_scale)
                act[rows] = (g / (1.0 + jnp.exp(-g)) * u).astype(BF16)

    sums_shape = (4 * ROWS, 2 * WIDTH + 128)
    extra = [] if carry is None else [carry]
    if last:
        out_specs, out_shape = fixed((4 * ROWS, WIDTH)), shape((4 * ROWS, WIDTH), BF16)
        scratch = [pltpu.VMEM(sums_shape, F32)]
    else:
        out_specs, out_shape, scratch = fixed(sums_shape), shape(sums_shape, F32), []
    return pl.pallas_call(
        body,
        grid=(1,),
        in_specs=[SMEM, SMEM] + [ANY] * (4 * many + 4 + len(extra)),
        out_specs=out_specs,
        out_shape=out_shape,
        scratch_shapes=scratch
        + [
            pltpu.VMEM((4 * many * ROWS, FEAT), BF16),
            pltpu.VMEM((4, 2 * WIDTH, FEAT), BF16),
            pltpu.SemaphoreType.DMA((4 * many,)),
            pltpu.SemaphoreType.DMA((4, 4)),
            pltpu.SemaphoreType.DMA,
        ],
        cost_estimate=pl.CostEstimate(
            flops=8 * many * ROWS * FEAT * 2 * WIDTH, bytes_accessed=20 << 20, transcendentals=0
        ),
        compiler_params=pltpu.CompilerParams(vmem_limit_bytes=ALL_VMEM),
        name=name,
    )(tab, scales, *blocks, *weights, *extra)


def down_call(tab, units, act, weights, name):
    many = len(units)

    def body(tab, act, wd, wdo, *refs):
        outs, (held, sem) = refs[: 4 * many], refs[4 * many :]
        core = tab[3]

        def copies(s, chip):
            cols = pl.ds(pl.multiple_of(chip * FEAT, FEAT), FEAT)
            return [
                pltpu.make_async_copy(
                    w.at[:, cols], held.at[s, pl.ds(at, SLICE)], sem.at[s, i]
                )
                for i, (w, at) in enumerate(((wd, 0), (wdo, SLICE)))
            ]

        for s in range(4):
            if s < many:
                for copy in copies(s, at_offset(tab, units[s], s)):
                    copy.start()
            else:

                @pl.when(core == 1)
                def _(s=s):
                    for copy in copies(s, at_offset(tab, s, s)):
                        copy.start()

            held[s, 2 * SLICE :] = jnp.zeros((WIDTH - 2 * SLICE, FEAT), BF16)

        @pl.when(core == 0)
        def _():
            for u in range(many):
                for copy in copies(u, 0):
                    copy.wait()
                made = dot(act[...], held[u]).astype(BF16)
                for j in range(4):
                    outs[4 * u + j][...] = made[j * ROWS : (j + 1) * ROWS]

        @pl.when(core == 1)
        def _():
            for j in range(4):
                for copy in copies(j, 0):
                    copy.wait()
                rows = slice(units[0] * ROWS, (units[0] + many) * ROWS)
                made = dot(act[rows], held[j]).astype(BF16)
                for u in range(many):
                    outs[4 * u + j][...] = made[u * ROWS : (u + 1) * ROWS]

    block = (ROWS, FEAT)
    return pl.pallas_call(
        body,
        grid=(1,),
        in_specs=[SMEM, fixed((4 * ROWS, WIDTH)), ANY, ANY],
        out_specs=[fixed(block)] * (4 * many),
        out_shape=[shape(block, BF16)] * (4 * many),
        scratch_shapes=[pltpu.VMEM((4, WIDTH, FEAT), BF16), pltpu.SemaphoreType.DMA((4, 2))],
        cost_estimate=pl.CostEstimate(
            flops=8 * many * ROWS * FEAT * WIDTH, bytes_accessed=10 << 20, transcendentals=0
        ),
        compiler_params=pltpu.CompilerParams(vmem_limit_bytes=ALL_VMEM),
        name=name,
    )(tab, act, *weights)


def added(*parts):
    return sum(p.astype(F32) for p in parts).astype(BF16)


def reduced_body(tab, scales, a, b, c, o0, o1, o2, o3):
    scale = scales[2 + 2 * EXPERTS + tab[0]] * FF ** (-0.5)
    total = (a[...].astype(F32) + b[...].astype(F32) + c[...].astype(F32)) * scale
    for r, out in enumerate((o0, o1, o2, o3)):
        out[...] = total[r * HALF : (r + 1) * HALF].astype(BF16)


def routed_body(tab, high, low, p0, p1, p2, p3, mine, other, made):
    rows = jnp.concatenate([p[...].astype(F32) for p in (p0, p1, p2, p3)], axis=0).astype(BF16)
    across = ((0,), (0,))
    made[...] = dot(by_distance(tab, high), rows, across) + dot(by_distance(tab, low), rows, across)
    for at, out in ((tab[3], mine), (1 - tab[3], other)):
        out[...] = made[:, pl.ds(pl.multiple_of(at * CORE, CORE), CORE)]


def local(
    queries,
    memory_keys,
    memory_values,
    log_decay,
    hidden_in,
    out_weight,
    routes,
    route_weight,
    gate_weight,
    up_weight,
    down_weight,
    scales,
):
    z, x, y, c = (lax.axis_index(a) for a in ("z", "x", "y", "c"))
    tab = jnp.stack([z, x, y, c]).astype(jnp.int32)
    log_decay, routes, route_weight = log_decay.T, routes.T, route_weight.T
    gate_weight, up_weight = gate_weight.T, up_weight.T

    gate_other, up_other, down_other = swap(gate_weight), swap(up_weight), swap(down_weight)

    piece = shape((272, 128), BF16)
    states = whole(
        states_body, [piece] * 4, [tab], [memory_keys, memory_values, log_decay], name="states"
    )
    sent = [states[0]] + [turn(states[r], "x", r) for r in (1, 2, 3)]
    held = pltpu.VMEM((4, 272, 128), BF16)
    (group,) = whole(group_body, [piece], [tab], sent, [held], name="group")
    groups = [turn(group, "z", r) for r in (1, 2, 3)]
    carried = whole(
        carried_body,
        [shape((256, 128), BF16)] * 4,
        [tab],
        [*sent, *groups],
        [held, pltpu.VMEM((4, 256, 128), BF16)],
        name="carried",
    )
    carried = [carried[0]] + [turn(carried[r], "x", r) for r in (1, 2, 3)]

    table = shape((EXPERTS, 2, HALF, TOKENS), F32)
    inside, chosen, high, low = whole(
        inside_body,
        [shape((TOKENS, 1024), F32), table, table, table],
        [],
        [queries, memory_keys, memory_values, log_decay, routes, route_weight],
        flops=4 * 8 * 128**3,
        name="inside",
    )
    heads_out, far = projected_first(tab, queries, inside, log_decay, carried, out_weight)
    far = swap(far)
    near = projected_second(tab, heads_out, out_weight)
    part = shape((TOKENS, CORE), BF16)
    parts = whole(
        joined_body, [shape((TOKENS, CORE), F32), part, part, part], [], [near, far], name="joined"
    )
    arrived = [turn(parts[k], "y", k) for k in (2, 1, 3)]
    resid, narrow = whole(
        resid_body,
        [shape((TOKENS, CORE), F32), part],
        [scales],
        [parts[0], *arrived, hidden_in],
        name="resid",
    )
    packed = whole(
        pack_body,
        [shape((HALF, FEAT), BF16)] * 4,
        [tab],
        [chosen, narrow, swap(narrow)],
        name="pack",
    )
    own = jnp.concatenate([packed[0]] + [turn(packed[r], "z", r) for r in (1, 2, 3)], axis=0)

    top, bottom = slice(0, HALF * 2), slice(HALF * 2, ROWS)
    left, right = ring(own, 1, 1), ring(own, 1, -1)
    own_l, own_r = ring(own, 2, 1), ring(own, 2, -1)
    far_block = jnp.concatenate([ring(left[top], 1, 1), ring(right[bottom], 1, -1)], axis=0)
    left_l, left_r = ring(left, 2, 1), ring(left, 2, -1)
    right_l, right_r = ring(right, 2, 1), ring(right, 2, -1)
    far_l, far_r = ring(far_block, 2, 1), ring(far_block, 2, -1)
    beyond = [ring(own_l, 2, 1), ring(left_l, 2, 1), ring(right_r, 2, -1), ring(far_r, 2, -1)]

    weights = (gate_weight, gate_other, up_weight, up_other)
    sums = hidden_call(
        tab, scales, (0,), [own, left, right, far_block], weights, None, False, "hidden_first"
    )
    middle = [own_l, left_l, right_l, far_l, own_r, left_r, right_r, far_r]
    sums = hidden_call(tab, scales, (1, 2), middle, weights, sums, False, "hidden_second")
    act = hidden_call(tab, scales, (3,), beyond, weights, sums, True, "hidden_third")

    downs = (down_weight, down_other)
    u_far = down_call(tab, (3,), act, downs, "down_far")
    rest = list(down_call(tab, (0, 1, 2), act, downs, "down_rest"))
    u_own, u_left, u_right = rest[:4], rest[4:8], rest[8:]
    for j in (1, 0):
        u_right[j] = added(u_right[j], ring(u_far[j], 2, 1))
    for j in (3, 2):
        u_left[j] = added(u_left[j], ring(u_far[j], 2, -1))
    blocks = {}
    for j in (3, 2, 1, 0):
        blocks[j] = (u_own[j], ring(u_right[j], 2, 1), ring(u_left[j], 2, -1))
    opposite = added(*blocks[3])
    from_left, from_right = ring(opposite[top], 1, 1), ring(opposite[bottom], 1, -1)
    to_right, to_left = added(*blocks[2]), added(*blocks[1])
    to_right = jnp.concatenate([added(to_right[top], from_left), to_right[bottom]], axis=0)
    to_left = jnp.concatenate([to_left[top], added(to_left[bottom], from_right)], axis=0)
    back = whole(
        reduced_body,
        [shape((HALF, FEAT), BF16)] * 4,
        [tab, scales],
        [added(*blocks[0]), ring(to_right, 1, 1), ring(to_left, 1, -1)],
        name="reduced",
    )
    home = [back[0]] + [turn(back[r], "z", -r) for r in (1, 2, 3)]
    wide = shape((TOKENS, CORE), F32)
    moe, moe_other = whole(routed_body, [wide, wide], [tab], [high, low, *home], [pltpu.VMEM((TOKENS, FEAT), F32)], name="routed")
    return (resid + moe + swap(moe_other)).astype(BF16)


def solution(mesh):
    torus = Mesh(mesh.devices.reshape(4, 4, 4, 2), ("z", "x", "y", "c"))
    return jax.shard_map(
        local,
        mesh=torus,
        in_specs=(
            P(SEQ, HEAD),
            P(SEQ, HEAD),
            P(SEQ, HEAD),
            P(SEQ, HEAD),
            P(SEQ, HEAD),
            P(HEAD, None),
            P(SEQ, None),
            P(SEQ, None),
            P(None, SEQ + HEAD),
            P(None, SEQ + HEAD),
            P(SEQ + HEAD, None),
            P(),
        ),
        out_specs=P(SEQ, HEAD),
        check_vma=False,
    )
```
